256 devices in a mesh: section: 4 (over x), tp: 64 (over y, z, core).
Axes of the slice: x: 4, y: 4, z: 8, core: 2. Of those that a mesh axis runs over, the one named last changes fastest.
Arguments:
- tokens: bfloat16 [64, 8192], P(None, 'tp'), may hold values from -6 to 6
- norm_gain: float32 [4, 8192], P('section'), may hold values from 0.1 to 1.9
- gate_weight: bfloat16 [4, 8192, 16384], P('section', None, 'tp'), may hold values from -0.09375 to 0.09375
- up_weight: bfloat16 [4, 8192, 16384], P('section', None, 'tp'), may hold values from -0.09375 to 0.09375
- gate_mask: int32 [4, 128, 256], P('section', None, 'tp'), may hold values 0 or 1
- up_mask: int32 [4, 128, 256], P('section', None, 'tp'), may hold values 0 or 1
- down_weight: bfloat16 [4, 16384, 8192], P('section', 'tp'), may hold values from -0.125 to 0.125
- down_mask: int32 [4, 256, 128], P('section', 'tp'), may hold values 0 or 1
- slot_order: int32 [4, 256], P('section', 'tp'), may hold values from 0 to 255, as said below
Outputs:
- received: bfloat16 [4, 64, 8192], P('section', None, 'tp')
The draws below stay inside these ranges and needn't reach their ends.
Inputs may be any that keep to these rules, and one draw needn't show every extreme that they name: `slot_order`: for each section a permutation of the 256 hidden blocks. Slot k lies on tp device k // 4; block b is computed on tp device b // 4. The slots of tp device t take exactly 1 block from each of the tp devices t, t + 1, ..., t + 4 - 1 (mod 64) and none from others. `gate_mask`: 1 keeps a block, 0 prunes it. `up_mask`: 1 keeps a block, 0 prunes it. `down_mask`: 1 keeps a block, 0 prunes it.
All inputs are finite; a program needn't handle non-finite values.
Results may differ from the reference program's by a relative error of at most 0.014.
Values may be sent and summed in bfloat16 or wider, within the bound.
A program may use at most 128 MiB of HBM per device.

```python
import jax
import jax.numpy as jnp
from jax import lax

D = 8192
FF = 16384
BLOCK = 64
ROWS = 64
NB = 256
BLK_DEV = 4
N_SECTION = 4
N_TP = 64


def draw_slot_order(key, part):
    window = min(N_TP, BLK_DEV)
    capacity = BLK_DEV // window

    def single(section_key):
        first_key, second_key = jax.random.split(section_key)
        given = jax.vmap(lambda sub_key: jax.random.permutation(sub_key, BLK_DEV))(jax.random.split(first_key, N_TP))
        lanes = jax.vmap(lambda sub_key: jax.random.permutation(sub_key, BLK_DEV))(jax.random.split(second_key, N_TP))
        target = jnp.arange(N_TP, dtype=jnp.int32)[:, None]
        offset = (lanes // capacity).astype(jnp.int32)
        source = (target + offset) % N_TP
        local_block = given[source, lanes]
        return (source * BLK_DEV + local_block).reshape(-1).astype(jnp.int32)
    return jax.vmap(single)(jax.random.split(key, N_SECTION))


def touch_ends(result, key, least, top_value):
    shape = result.shape
    index_at = [jax.random.randint(jax.random.fold_in(key, axis), (), 0, shape[axis]) for axis in range(len(shape))]
    result = result.at[tuple(index_at)].set(least)
    longest = shape.index(max(shape))
    index_at[longest] = (index_at[longest] + 1) % shape[longest]
    return result.at[tuple(index_at)].set(top_value)


def shard_levels(stream_key, dims, cuts, low, top_value):
    def one(axis_at, parts):
        heights = jax.random.uniform(jax.random.fold_in(jax.random.fold_in(stream_key, 6), axis_at), (parts,), jnp.float32, low / len(cuts), top_value / len(cuts))
        return jnp.repeat(jnp.exp(heights), dims[axis_at] // parts).reshape((-1,) + (1,) * (len(dims) - axis_at - 1))

    factor_of = one(*cuts[0])
    for cut in cuts[1:]:
        factor_of = factor_of * one(*cut)
    return factor_of


def noise(own_key, dims, width, most, cuts=(), kind=jnp.bfloat16):
    array = width * jax.random.normal(own_key, dims, jnp.float32)
    if cuts:
        array = array * shard_levels(own_key, dims, cuts, -0.22, 0.18)
    return jnp.clip(array, -most, most).astype(kind)


def setup_inputs(seed: int = 0) -> dict:
    streams_of = jax.random.split(jax.random.key(seed), 10)
    return {
        "tokens": noise(streams_of[0], (ROWS, D), 1.0, 6.0, ((1, 64),)),
        "norm_gain": jnp.clip(1.0 + 0.18 * jax.random.normal(streams_of[1], (N_SECTION, D), jnp.float32), 0.1, 1.9),
        "gate_weight": noise(streams_of[2], (N_SECTION, D, FF), (D // 2) ** -0.5, 0.09375, ((0, 4), (2, 64))),
        "up_weight": noise(streams_of[3], (N_SECTION, D, FF), (D // 2) ** -0.5, 0.09375, ((0, 4), (2, 64))),
        "gate_mask": touch_ends((jax.random.randint(streams_of[4], (N_SECTION, D // BLOCK, NB), 0, 2) < 1).astype(jnp.int32), jax.random.fold_in(streams_of[4], 1), 0, 1),
        "up_mask": touch_ends((jax.random.randint(streams_of[5], (N_SECTION, D // BLOCK, NB), 0, 2) < 1).astype(jnp.int32), jax.random.fold_in(streams_of[5], 1), 0, 1),
        "down_weight": noise(streams_of[6], (N_SECTION, FF, D), (FF // 8) ** -0.5, 0.125, ((0, 4), (1, 64))),
        "down_mask": touch_ends((jax.random.randint(streams_of[7], (N_SECTION, NB, D // BLOCK), 0, 2) < 1).astype(jnp.int32), jax.random.fold_in(streams_of[7], 1), 0, 1),
        "slot_order": draw_slot_order(jax.random.fold_in(streams_of[9], 71), 0),
    }


def expand_mask(mask):
    return jnp.repeat(jnp.repeat(mask, BLOCK, axis=0), BLOCK, axis=1)

def masked(weight, mask):
    return weight * expand_mask(mask).astype(jnp.bfloat16)

def layer(inputs, gain, gate_weight, up_weight, gate_mask, up_mask, down_weight, down_mask, order):
    widened = inputs.astype(jnp.float32)
    scale = jax.lax.rsqrt(lax.optimization_barrier(jnp.mean(widened * widened, axis=-1, keepdims=True)) + 1e-05)
    normed = (widened * scale * gain).astype(jnp.bfloat16)
    gate = jnp.dot(normed, masked(gate_weight, gate_mask), preferred_element_type=jnp.float32)
    upper = jnp.dot(normed, masked(up_weight, up_mask), preferred_element_type=jnp.float32)
    hidden = (jax.nn.silu(gate) * upper).astype(jnp.bfloat16)
    tiles = hidden.reshape(ROWS, NB, BLOCK)[:, order.astype(jnp.int32), :].reshape(ROWS, FF)
    summed = jnp.dot(tiles, masked(down_weight, down_mask), preferred_element_type=jnp.float32)
    return (widened + summed).astype(jnp.bfloat16)

def reference(tokens, norm_gain, gate_weight, up_weight, gate_mask, up_mask, down_weight, down_mask, slot_order):
    current = tokens
    results = [None] * N_SECTION
    for layer_pos in range(N_SECTION):
        current = layer(current, norm_gain[layer_pos], gate_weight[layer_pos], up_weight[layer_pos], gate_mask[layer_pos], up_mask[layer_pos], down_weight[layer_pos], down_mask[layer_pos], slot_order[layer_pos])
        results[(layer_pos + 1) % N_SECTION] = current
    return jnp.stack(results)
```

```python
import functools

import jax
import jax.numpy as jnp
from jax import lax
from jax.experimental import pallas as pl
from jax.experimental.pallas import tpu as pltpu
from jax.sharding import PartitionSpec as P

MESH = pl.DeviceIdType.MESH
BF = jnp.bfloat16
F32 = jnp.float32
REACH = 4
GROUP = 4


def tp_grid(count):
    ny = {64: 4, 32: 4, 16: 2, 8: 2}[count]
    return ny, count // (2 * ny)


def kernel(
    sections,
    ny,
    nz,
    tokens_h,
    gain_h,
    wg_h,
    wu_h,
    gm_h,
    um_h,
    wd_h,
    dm_h,
    so_h,
    out_ref,
    wg,
    wu,
    wd,
    wdp,
    gain,
    gm,
    um,
    dm,
    so_v,
    gme,
    ume,
    perm,
    xbuf,
    xprev,
    hsend,
    hrecv,
    part,
    psend,
    precv,
    ysend,
    yrecv,
    zsend,
    zrecv,
    lsem,
    so_ss,
    so_rs,
    az_ss,
    az_rs,
    ay_ss,
    ay_rs,
    ap_ss,
    ap_rs,
    h_ss,
    h_rs,
    p_ss,
    p_rs,
    y_ss,
    y_rs,
    z_ss,
    z_rs,
    x_ss,
    x_rs,
):
    nt = ny * nz * 2
    rows = tokens_h.shape[0]
    feats = nt * 128
    groups = nz // GROUP
    s = lax.axis_index("section")
    t = lax.axis_index("tp")
    c = t % 2
    chip = t // 2
    z = chip % nz
    y = chip // nz
    s_next = (s + 1) % sections
    s_last = (s + sections - 1) % sections
    far = [nz // 2 + p // 2 if p % 2 == 0 else nz // 2 - 1 - p // 2 for p in range(nz)]
    near = far[::-1]
    y_far = [ny // 2] + [d for d in range(1, ny) if d != ny // 2]

    def pos(yy, zz):
        return (yy % ny) * nz + zz % nz

    def tp_of(yy, zz, cc):
        return pos(yy, zz) * 2 + cc

    partner = t + 1 - 2 * c

    def remote(src, dst, ss, rs, sec, tp):
        return pltpu.make_async_remote_copy(
            src_ref=src,
            dst_ref=dst,
            send_sem=ss,
            recv_sem=rs,
            device_id=(sec, tp),
            device_id_type=MESH,
        )

    loads = [
        pltpu.make_async_copy(src, dst, lsem.at[i])
        for i, (src, dst) in enumerate(
            [
                (so_h, so_v.at[0]),
                (gm_h, gm),
                (um_h, um),
                (dm_h, dm),
                (gain_h, gain),
                (wg_h, wg),
                (wu_h, wu),
                (wd_h, wd),
            ]
        )
    ]
    for one in loads:
        one.start()
    token_load = pltpu.make_async_copy(tokens_h, xbuf.at[0, 0, c], lsem.at[9])

    @pl.when(s == 0)
    def _():
        token_load.start()

    barrier = pltpu.get_barrier_semaphore()
    peers = [(s, partner)]
    peers += [(s, tp_of(y + d, z, c)) for d in range(1, ny)]
    peers += [(s, tp_of(y, z + d, c)) for d in range(1, nz)]
    peers += [(s, (t + d) % nt) for d in range(1, REACH)]
    peers += [(s, (t + nt - d) % nt) for d in range(1, REACH)]
    peers += [(s_next, tp_of(y, z + d, c)) for d in range(nz)]
    peers += [(s_last, tp_of(y, z + d, c)) for d in range(nz)]
    for peer in peers:
        pl.semaphore_signal(barrier, inc=1, device_id=peer, device_id_type=MESH)
    pl.semaphore_wait(barrier, len(peers))

    for one in loads[:5]:
        one.wait()
    so_copies = [
        remote(so_v.at[0], so_v.at[j], so_ss.at[j], so_rs.at[j], s, (t + j) % nt)
        for j in range(1, REACH)
    ]
    for one in so_copies:
        one.start()

    own = xbuf.at[0, 0, c]

    def z_gather(d):
        return remote(
            own, xbuf.at[0, d, c], az_ss.at[d], az_rs.at[d], s, tp_of(y, z + d, c)
        )

    def y_gather(dy, d):
        return remote(
            xbuf.at[0, d, c],
            xbuf.at[dy, d, c],
            ay_ss.at[dy, d],
            ay_rs.at[dy, d],
            s,
            tp_of(y + dy, z, c),
        )

    def p_gather(dy, d):
        return remote(
            xbuf.at[dy, d, c],
            xbuf.at[dy, d, c],
            ap_ss.at[dy, d],
            ap_rs.at[dy, d],
            s,
            partner,
        )

    keep_copy = remote(own, xprev, x_ss.at[0], x_rs.at[0], s_next, t)

    def z_scatter(p):
        return remote(
            zsend.at[p],
            zrecv.at[p],
            z_ss.at[p],
            z_rs.at[p],
            s_next,
            tp_of(y, z + far[p], c),
        )

    def send_own():
        for d in far[:-1]:
            z_gather(d).start()
        for dy in y_far:
            y_gather(dy, 0).start()
        p_gather(0, 0).start()
        keep_copy.start()

    def arrive():
        keep_copy.wait_recv()
        total = xprev[...].astype(F32)
        for p in range(nz):
            z_scatter(p).wait_recv()
            total = total + zrecv[p].astype(F32)
        return total.astype(BF)

    @pl.when(s == 0)
    def _():
        token_load.wait()
        send_own()

    spread_at = lax.broadcasted_iota(jnp.int32, (4, 256), 1) // 64
    spread_of = lax.broadcasted_iota(jnp.int32, (4, 256), 0)
    spread = jnp.where(spread_at == spread_of, 1.0, 0.0).astype(BF)
    for raw, wide in ((gm, gme), (um, ume)):
        wide[...] = lax.dot_general(
            raw[...].astype(BF),
            spread,
            (((0,), (0,)), ((), ())),
            preferred_element_type=F32,
        )

    def mask_up(weight, wide):
        @pl.loop(0, feats // 64)
        def _(i):
            at = pl.ds(pl.multiple_of(i * 64, 64), 64)
            row = jnp.broadcast_to(wide[pl.ds(i, 1), :], (16, 256)).astype(BF)
            block = weight[at, :].reshape(4, 16, 256) * row[None]
            weight[at, :] = block.reshape(64, 256)

    loads[5].wait()
    mask_up(wg, gme)
    loads[6].wait()
    mask_up(wu, ume)

    down_bits = dm[...].astype(BF)
    pick_row = lax.broadcasted_iota(jnp.int32, (feats // 64, 256), 0)
    pick_lane = lax.broadcasted_iota(jnp.int32, (feats // 64, 256), 1) // 64
    sort_row = lax.broadcasted_iota(jnp.int32, (256, 256), 0)
    sort_lane = lax.broadcasted_iota(jnp.int32, (256, 256), 1)
    sender = (so_v[0] // 4 + nt - t) % nt
    sender_of = jnp.zeros((1, 256), jnp.int32)
    for k in range(REACH):
        sender_of = jnp.where(
            sort_lane[:1] // 64 == k, sender[:, k : k + 1], sender_of
        )
    same = (sort_row // 64 == sender_of) & (sort_row % 64 == sort_lane % 64)
    sort = jnp.where(same, 1.0, 0.0).astype(BF)

    loads[7].wait()

    @pl.loop(0, feats // 256)
    def _(i):
        cols = pl.ds(pl.multiple_of(i * 256, 256), 256)
        pick = jnp.where(pick_row == 4 * i + pick_lane, 1.0, 0.0).astype(BF)
        bits = jnp.dot(down_bits, pick, preferred_element_type=F32)
        blocks = []
        for k in range(REACH):
            row = jnp.broadcast_to(bits[k : k + 1], (16, 256)).astype(BF)
            block = wd[k * 64 : (k + 1) * 64, cols].reshape(4, 16, 256) * row[None]
            blocks.append(block.reshape(64, 256))
        wdp[:, cols] = jnp.dot(
            sort, jnp.concatenate(blocks, axis=0), preferred_element_type=F32
        ).astype(BF)

    for one in so_copies:
        one.wait_recv()
    row_of = lax.broadcasted_iota(jnp.int32, (256, 128), 0)
    lane_of = lax.broadcasted_iota(jnp.int32, (256, 128), 1)
    for j in range(REACH):
        order = so_v[j]
        mine = jnp.sum(
            jnp.where(order // 4 == t, order % 4, 0), axis=1, keepdims=True
        )
        hit = (row_of == mine * 64 + lane_of % 64) & (lane_of // 64 == j % 2)
        perm[:, j * 128 : (j + 1) * 128] = jnp.where(hit, 1.0, 0.0).astype(BF)

    @pl.when(s > 0)
    def _():
        rows_in = arrive()
        xbuf[0, 0, c] = rows_in
        out_ref[...] = rows_in
        send_own()

    def block_product(d, state):
        gate, upper, squares = state
        for dy in range(ny):
            at = pos(y + ny - dy, z + nz - d)
            wide = jnp.concatenate(
                [xbuf[dy, d, 0], xbuf[dy, d, 1]], axis=1
            ).astype(F32)
            squares = squares + wide * wide
            where = pl.ds(pl.multiple_of(at * 256, 256), 256)
            left = (wide * gain[:, where]).astype(BF)
            gate = gate + jnp.dot(left, wg[where, :], preferred_element_type=F32)
            upper = upper + jnp.dot(left, wu[where, :], preferred_element_type=F32)
        return gate, upper, squares

    state = tuple(jnp.zeros((rows, 256), F32) for _ in range(3))
    for step in range(nz + 2):
        if 1 <= step < nz:
            d = near[step]
            z_gather(d).wait_recv()
            for dy in y_far:
                y_gather(dy, d).start()
            p_gather(0, d).start()
        if 1 <= step <= nz:
            d = near[step - 1]
            for dy in y_far[::-1]:
                y_gather(dy, d).wait_recv()
                p_gather(dy, d).start()
        if step >= 2:
            d = near[step - 2]
            for dy in range(ny):
                remote(
                    xbuf.at[dy, d, c],
                    xbuf.at[dy, d, 1 - c],
                    ap_ss.at[dy, d],
                    ap_rs.at[dy, d],
                    s,
                    partner,
                ).wait_recv()
            state = block_product(d, state)
    gate, upper, squares = state
    scale = lax.rsqrt(jnp.sum(squares, axis=1, keepdims=True) / feats + 1e-05)
    gate = gate * scale
    hidden = (gate / (1.0 + jnp.exp(-gate)) * (upper * scale)).astype(BF)
    routed = jnp.dot(hidden, perm[...], preferred_element_type=F32).astype(BF)

    def hand_over(j):
        return remote(
            hsend.at[j], hrecv.at[j], h_ss.at[j], h_rs.at[j], s, (t + nt - j) % nt
        )

    for j in range(REACH - 1, 0, -1):
        hsend[j] = routed[:, j * 128 : (j + 1) * 128]
        hand_over(j).start()
    for j in range(1, REACH):
        hand_over(j).wait_recv()
    tiles = jnp.concatenate(
        [routed[:, :128] + hrecv[1], hrecv[2] + hrecv[3]], axis=1
    )

    def p_scatter(g):
        some = pl.ds(g * GROUP, GROUP)
        return remote(
            psend.at[some], precv.at[some], p_ss.at[g], p_rs.at[g], s, partner
        )

    def y_scatter(dy, g):
        some = pl.ds(g * GROUP, GROUP)
        return remote(
            ysend.at[dy, some],
            yrecv.at[dy, some],
            y_ss.at[dy, g],
            y_rs.at[dy, g],
            s,
            tp_of(y + dy, z, c),
        )

    for g in range(groups):
        for p in range(g * GROUP, (g + 1) * GROUP):
            for dy in range(ny):
                at = pos(y + dy, z + far[p])
                cols = pl.ds(pl.multiple_of(at * 256, 256), 256)
                both = jnp.dot(tiles, wdp[:, cols], preferred_element_type=F32)
                low, high = both[:, :128], both[:, 128:]
                part[p, dy] = jnp.where(c == 0, low, high)
                psend[p, dy] = jnp.where(c == 0, high, low).astype(BF)
        p_scatter(g).start()
    for g in range(groups):
        p_scatter(g).wait_recv()
        for dy in y_far:
            for p in range(g * GROUP, (g + 1) * GROUP):
                ysend[dy, p] = (part[p, dy] + precv[p, dy].astype(F32)).astype(BF)
            y_scatter(dy, g).start()
    for g in range(groups):
        for dy in y_far[::-1]:
            y_scatter(dy, g).wait_recv()
        for p in range(g * GROUP, (g + 1) * GROUP):
            total = part[p, 0] + precv[p, 0].astype(F32)
            for dy in range(1, ny):
                total = total + yrecv[dy, p].astype(F32)
            zsend[p] = total.astype(BF)
            z_scatter(p).start()

    @pl.when(s == 0)
    def _():
        out_ref[...] = arrive()

    for one in so_copies:
        one.wait_send()
    keep_copy.wait_send()
    for d in range(1, nz):
        z_gather(d).wait_send()
    for d in range(nz):
        for dy in range(1, ny):
            y_gather(dy, d).wait_send()
        for dy in range(ny):
            p_gather(dy, d).wait_send()
        z_scatter(d).wait_send()
    for j in range(1, REACH):
        hand_over(j).wait_send()
    for g in range(groups):
        p_scatter(g).wait_send()
        for dy in range(1, ny):
            y_scatter(dy, g).wait_send()


def body(
    tokens,
    norm_gain,
    gate_weight,
    up_weight,
    gate_mask,
    up_mask,
    down_weight,
    down_mask,
    slot_order,
):
    sections = lax.axis_size("section")
    nt = lax.axis_size("tp")
    ny, nz = tp_grid(nt)
    rows = tokens.shape[0]
    feats = nt * 128
    groups = nz // GROUP
    dma = pltpu.SemaphoreType.DMA
    scratch = [
        pltpu.VMEM((feats, 256), BF),
        pltpu.VMEM((feats, 256), BF),
        pltpu.VMEM((256, feats), BF),
        pltpu.VMEM((256, feats), BF),
        pltpu.VMEM((1, feats), F32),
        pltpu.VMEM((4, feats // 64), jnp.int32),
        pltpu.VMEM((4, feats // 64), jnp.int32),
        pltpu.VMEM((4, feats // 64), jnp.int32),
        pltpu.VMEM((REACH, 1, 4), jnp.int32),
        pltpu.VMEM((feats // 64, 256), F32),
        pltpu.VMEM((feats // 64, 256), F32),
        pltpu.VMEM((256, REACH * 128), BF),
        pltpu.VMEM((ny, nz, 2, rows, 128), BF),
        pltpu.VMEM((rows, 128), BF),
        pltpu.VMEM((REACH, rows, 128), BF),
        pltpu.VMEM((REACH, rows, 128), BF),
        pltpu.VMEM((nz, ny, rows, 128), F32),
        pltpu.VMEM((nz, ny, rows, 128), BF),
        pltpu.VMEM((nz, ny, rows, 128), BF),
        pltpu.VMEM((ny, nz, rows, 128), BF),
        pltpu.VMEM((ny, nz, rows, 128), BF),
        pltpu.VMEM((nz, rows, 128), BF),
        pltpu.VMEM((nz, rows, 128), BF),
        dma((10,)),
    ]
    for shape in (
        (REACH,),
        (nz,),
        (ny, nz),
        (ny, nz),
        (REACH,),
        (groups,),
        (ny, groups),
        (nz,),
        (1,),
    ):
        scratch += [dma(shape), dma(shape)]
    received = pl.pallas_call(
        functools.partial(kernel, sections, ny, nz),
        out_shape=jax.ShapeDtypeStruct((rows, 128), BF),
        in_specs=[pl.BlockSpec(memory_space=pl.ANY)] * 9,
        out_specs=pl.BlockSpec(memory_space=pltpu.VMEM),
        scratch_shapes=scratch,
        compiler_params=pltpu.CompilerParams(
            collective_id=0,
            has_side_effects=True,
            vmem_limit_bytes=50 * 1024 * 1024,
        ),
    )(
        tokens,
        norm_gain,
        gate_weight[0],
        up_weight[0],
        gate_mask[0].T,
        up_mask[0].T,
        down_weight[0],
        down_mask[0],
        slot_order,
    )
    return received[None]


def solution(mesh):
    return jax.shard_map(
        body,
        mesh=mesh,
        in_specs=(
            P(None, "tp"),
            P("section", None),
            P("section", None, "tp"),
            P("section", None, "tp"),
            P("section", None, "tp"),
            P("section", None, "tp"),
            P("section", "tp", None),
            P("section", "tp", None),
            P("section", "tp"),
        ),
        out_specs=P("section", None, "tp"),
        check_vma=False,
    )
```

```python
import functools

import jax
import jax.numpy as jnp
from jax import lax
from jax.experimental import pallas as pl
from jax.experimental.pallas import tpu as pltpu
from jax.sharding import PartitionSpec as P

MESH = pl.DeviceIdType.MESH
BF = jnp.bfloat16
F32 = jnp.float32
REACH = 4
GROUP = 2


def tp_grid(count):
    ny = {64: 4, 32: 4, 16: 2, 8: 2}[count]
    return ny, count // (2 * ny)


def kernel(
    sections,
    ny,
    nz,
    tokens_h,
    gain_h,
    wg_h,
    wu_h,
    gm_h,
    um_h,
    wd_h,
    dm_h,
    so_h,
    out_ref,
    wg,
    wu,
    wd,
    wdp,
    gain,
    gm,
    um,
    dm,
    so_v,
    gme,
    ume,
    perm,
    xbuf,
    xprev,
    hsend,
    hrecv,
    part,
    psend,
    precv,
    ysend,
    yrecv,
    zsend,
    zrecv,
    lsem,
    so_ss,
    so_rs,
    az_ss,
    az_rs,
    ay_ss,
    ay_rs,
    ap_ss,
    ap_rs,
    h_ss,
    h_rs,
    p_ss,
    p_rs,
    y_ss,
    y_rs,
    z_ss,
    z_rs,
    x_ss,
    x_rs,
):
    nt = ny * nz * 2
    rows = tokens_h.shape[0]
    feats = nt * 128
    groups = nz // GROUP
    s = lax.axis_index("section")
    t = lax.axis_index("tp")
    c = t % 2
    chip = t // 2
    z = chip % nz
    y = chip // nz
    s_next = (s + 1) % sections
    s_last = (s + sections - 1) % sections
    far = [nz // 2 + p // 2 if p % 2 == 0 else nz // 2 - 1 - p // 2 for p in range(nz)]
    near = far[::-1]
    y_far = [ny // 2] + [d for d in range(1, ny) if d != ny // 2]

    def pos(yy, zz):
        return (yy % ny) * nz + zz % nz

    def tp_of(yy, zz, cc):
        return pos(yy, zz) * 2 + cc

    partner = t + 1 - 2 * c

    def remote(src, dst, ss, rs, sec, tp):
        return pltpu.make_async_remote_copy(
            src_ref=src,
            dst_ref=dst,
            send_sem=ss,
            recv_sem=rs,
            device_id=(sec, tp),
            device_id_type=MESH,
        )

    loads = [
        pltpu.make_async_copy(src, dst, lsem.at[i])
        for i, (src, dst) in enumerate(
            [
                (so_h, so_v.at[0]),
                (gm_h, gm),
                (um_h, um),
                (dm_h, dm),
                (gain_h, gain),
                (wg_h, wg),
                (wu_h, wu),
                (wd_h, wd),
            ]
        )
    ]
    for one in loads:
        one.start()
    token_load = pltpu.make_async_copy(tokens_h, xbuf.at[0, 0, c], lsem.at[9])

    @pl.when(s == 0)
    def _():
        token_load.start()

    barrier = pltpu.get_barrier_semaphore()
    peers = [(s, partner)]
    peers += [(s, tp_of(y + d, z, c)) for d in range(1, ny)]
    peers += [(s, tp_of(y, z + d, c)) for d in range(1, nz)]
    peers += [(s, (t + d) % nt) for d in range(1, REACH)]
    peers += [(s, (t + nt - d) % nt) for d in range(1, REACH)]
    peers += [(s_next, tp_of(y, z + d, c)) for d in range(nz)]
    peers += [(s_last, tp_of(y, z + d, c)) for d in range(nz)]
    for peer in peers:
        pl.semaphore_signal(barrier, inc=1, device_id=peer, device_id_type=MESH)

    for one in loads[:5]:
        one.wait()

    spread_at = lax.broadcasted_iota(jnp.int32, (4, 256), 1) // 64
    spread_of = lax.broadcasted_iota(jnp.int32, (4, 256), 0)
    spread = jnp.where(spread_at == spread_of, 1.0, 0.0).astype(BF)
    for raw, wide in ((gm, gme), (um, ume)):
        wide[...] = lax.dot_general(
            raw[...].astype(BF),
            spread,
            (((0,), (0,)), ((), ())),
            preferred_element_type=F32,
        )

    def mask_up(weight, wide):
        @pl.loop(0, feats // 64, unroll=8)
        def _(i):
            at = pl.ds(pl.multiple_of(i * 64, 64), 64)
            row = jnp.broadcast_to(wide[pl.ds(i, 1), :], (16, 256)).astype(BF)
            block = weight[at, :].reshape(4, 16, 256) * row[None]
            weight[at, :] = block.reshape(64, 256)

    loads[5].wait()
    mask_up(wg, gme)
    loads[6].wait()
    mask_up(wu, ume)

    down_bits = dm[...].astype(BF)
    pick_row = lax.broadcasted_iota(jnp.int32, (feats // 64, 256), 0)
    pick_lane = lax.broadcasted_iota(jnp.int32, (feats // 64, 256), 1) // 64
    sort_row = lax.broadcasted_iota(jnp.int32, (256, 256), 0)
    sort_lane = lax.broadcasted_iota(jnp.int32, (256, 256), 1)
    sender = (so_v[0] // 4 + nt - t) % nt
    sender_of = jnp.zeros((1, 256), jnp.int32)
    for k in range(REACH):
        sender_of = jnp.where(
            sort_lane[:1] // 64 == k, sender[:, k : k + 1], sender_of
        )
    same = (sort_row // 64 == sender_of) & (sort_row % 64 == sort_lane % 64)
    sort = jnp.where(same, 1.0, 0.0).astype(BF)

    def mask_down(first, last):
        @pl.loop(first, last, unroll=2)
        def _(i):
            cols = pl.ds(pl.multiple_of(i * 256, 256), 256)
            pick = jnp.where(pick_row == 4 * i + pick_lane, 1.0, 0.0).astype(BF)
            bits = jnp.dot(down_bits, pick, preferred_element_type=F32)
            blocks = []
            for k in range(REACH):
                row = jnp.broadcast_to(bits[k : k + 1], (16, 256)).astype(BF)
                block = wd[k * 64 : (k + 1) * 64, cols]
                block = block.reshape(4, 16, 256) * row[None]
                blocks.append(block.reshape(64, 256))
            wdp[:, cols] = jnp.dot(
                sort, jnp.concatenate(blocks, axis=0), preferred_element_type=F32
            ).astype(BF)

    tiles_down = feats // 256
    early, middle = tiles_down * 3 // 16 * 2, tiles_down * 5 // 16 * 2
    loads[7].wait()
    mask_down(0, early)

    pl.semaphore_wait(barrier, len(peers))

    own = xbuf.at[0, 0, c]

    def z_gather(d):
        return remote(
            own, xbuf.at[0, d, c], az_ss.at[d], az_rs.at[d], s, tp_of(y, z + d, c)
        )

    def y_gather(dy, d):
        return remote(
            xbuf.at[0, d, c],
            xbuf.at[dy, d, c],
            ay_ss.at[dy, d],
            ay_rs.at[dy, d],
            s,
            tp_of(y + dy, z, c),
        )

    def p_gather(dy, d):
        return remote(
            xbuf.at[dy, d, c],
            xbuf.at[dy, d, c],
            ap_ss.at[dy, d],
            ap_rs.at[dy, d],
            s,
            partner,
        )

    keep_copy = remote(own, xprev, x_ss.at[0], x_rs.at[0], s_next, t)

    def z_scatter(p):
        return remote(
            zsend.at[p],
            zrecv.at[p],
            z_ss.at[p],
            z_rs.at[p],
            s_next,
            tp_of(y, z + far[p], c),
        )

    def send_own():
        for d in far[:-1]:
            z_gather(d).start()
        for dy in y_far:
            y_gather(dy, 0).start()
        p_gather(0, 0).start()
        keep_copy.start()

    def arrive():
        keep_copy.wait_recv()
        total = xprev[...].astype(F32)
        for p in range(nz):
            z_scatter(p).wait_recv()
            total = total + zrecv[p].astype(F32)
        return total.astype(BF)

    @pl.when(s == 0)
    def _():
        token_load.wait()
        send_own()

    so_copies = [
        remote(so_v.at[0], so_v.at[j], so_ss.at[j], so_rs.at[j], s, (t + j) % nt)
        for j in range(1, REACH)
    ]
    for one in so_copies:
        one.start()

    mask_down(early, middle)

    for one in so_copies:
        one.wait_recv()
    row_of = lax.broadcasted_iota(jnp.int32, (256, 128), 0)
    lane_of = lax.broadcasted_iota(jnp.int32, (256, 128), 1)
    for j in range(REACH):
        order = so_v[j]
        mine = jnp.sum(
            jnp.where(order // 4 == t, order % 4, 0), axis=1, keepdims=True
        )
        hit = (row_of == mine * 64 + lane_of % 64) & (lane_of // 64 == j % 2)
        perm[:, j * 128 : (j + 1) * 128] = jnp.where(hit, 1.0, 0.0).astype(BF)

    @pl.when(s > 0)
    def _():
        mask_down(middle, tiles_down)
        rows_in = arrive()
        xbuf[0, 0, c] = rows_in
        out_ref[...] = rows_in
        send_own()

    def block_product(d, state):
        gate, upper, squares = state
        for dy in range(ny):
            at = pos(y + ny - dy, z + nz - d)
            wide = jnp.concatenate(
                [xbuf[dy, d, 0], xbuf[dy, d, 1]], axis=1
            ).astype(F32)
            squares = squares + wide * wide
            where = pl.ds(pl.multiple_of(at * 256, 256), 256)
            left = (wide * gain[:, where]).astype(BF)
            gate = gate + jnp.dot(left, wg[where, :], preferred_element_type=F32)
            upper = upper + jnp.dot(left, wu[where, :], preferred_element_type=F32)
        return gate, upper, squares

    state = tuple(jnp.zeros((rows, 256), F32) for _ in range(3))
    for d in near[1:]:
        z_gather(d).wait_recv()
        for dy in y_far:
            y_gather(dy, d).start()
        p_gather(0, d).start()

    @pl.when(s == 0)
    def _():
        mask_down(middle, tiles_down)

    for step in range(nz + 1):
        if step < nz:
            d = near[step]
            for dy in y_far[::-1]:
                y_gather(dy, d).wait_recv()
                p_gather(dy, d).start()
        if step >= 1:
            d = near[step - 1]
            for dy in range(ny):
                remote(
                    xbuf.at[dy, d, c],
                    xbuf.at[dy, d, 1 - c],
                    ap_ss.at[dy, d],
                    ap_rs.at[dy, d],
                    s,
                    partner,
                ).wait_recv()
            state = block_product(d, state)
    gate, upper, squares = state
    scale = lax.rsqrt(jnp.sum(squares, axis=1, keepdims=True) / feats + 1e-05)
    gate = gate * scale
    hidden = (gate / (1.0 + jnp.exp(-gate)) * (upper * scale)).astype(BF)
    routed = jnp.dot(hidden, perm[...], preferred_element_type=F32).astype(BF)

    def hand_over(j):
        return remote(
            hsend.at[j], hrecv.at[j], h_ss.at[j], h_rs.at[j], s, (t + nt - j) % nt
        )

    for j in range(REACH - 1, 0, -1):
        hsend[j] = routed[:, j * 128 : (j + 1) * 128]
        hand_over(j).start()
    for j in range(1, REACH):
        hand_over(j).wait_recv()
    tiles = jnp.concatenate(
        [routed[:, :128] + hrecv[1], hrecv[2] + hrecv[3]], axis=1
    )

    def p_scatter(g):
        some = pl.ds(g * GROUP, GROUP)
        return remote(
            psend.at[some], precv.at[some], p_ss.at[g], p_rs.at[g], s, partner
        )

    def y_scatter(dy, g):
        some = pl.ds(g * GROUP, GROUP)
        return remote(
            ysend.at[dy, some],
            yrecv.at[dy, some],
            y_ss.at[dy, g],
            y_rs.at[dy, g],
            s,
            tp_of(y + dy, z, c),
        )

    for g in range(groups):
        for p in range(g * GROUP, (g + 1) * GROUP):
            for dy in range(ny):
                at = pos(y + dy, z + far[p])
                cols = pl.ds(pl.multiple_of(at * 256, 256), 256)
                both = jnp.dot(tiles, wdp[:, cols], preferred_element_type=F32)
                low, high = both[:, :128], both[:, 128:]
                part[p, dy] = jnp.where(c == 0, low, high)
                psend[p, dy] = jnp.where(c == 0, high, low).astype(BF)
        p_scatter(g).start()
    for g in range(groups):
        p_scatter(g).wait_recv()
        for dy in y_far:
            for p in range(g * GROUP, (g + 1) * GROUP):
                ysend[dy, p] = (part[p, dy] + precv[p, dy].astype(F32)).astype(BF)
            y_scatter(dy, g).start()
    for g in range(groups):
        for dy in y_far[::-1]:
            y_scatter(dy, g).wait_recv()
        for p in range(g * GROUP, (g + 1) * GROUP):
            total = part[p, 0] + precv[p, 0].astype(F32)
            for dy in range(1, ny):
                total = total + yrecv[dy, p].astype(F32)
            zsend[p] = total.astype(BF)
            z_scatter(p).start()

    @pl.when(s == 0)
    def _():
        out_ref[...] = arrive()

    for one in so_copies:
        one.wait_send()
    keep_copy.wait_send()
    for d in range(1, nz):
        z_gather(d).wait_send()
    for d in range(nz):
        for dy in range(1, ny):
            y_gather(dy, d).wait_send()
        for dy in range(ny):
            p_gather(dy, d).wait_send()
        z_scatter(d).wait_send()
    for j in range(1, REACH):
        hand_over(j).wait_send()
    for g in range(groups):
        p_scatter(g).wait_send()
        for dy in range(1, ny):
            y_scatter(dy, g).wait_send()


def body(
    tokens,
    norm_gain,
    gate_weight,
    up_weight,
    gate_mask,
    up_mask,
    down_weight,
    down_mask,
    slot_order,
):
    sections = lax.axis_size("section")
    nt = lax.axis_size("tp")
    ny, nz = tp_grid(nt)
    rows = tokens.shape[0]
    feats = nt * 128
    groups = nz // GROUP
    dma = pltpu.SemaphoreType.DMA
    scratch = [
        pltpu.VMEM((feats, 256), BF),
        pltpu.VMEM((feats, 256), BF),
        pltpu.VMEM((256, feats), BF),
        pltpu.VMEM((256, feats), BF),
        pltpu.VMEM((1, feats), F32),
        pltpu.VMEM((4, feats // 64), jnp.int32),
        pltpu.VMEM((4, feats // 64), jnp.int32),
        pltpu.VMEM((4, feats // 64), jnp.int32),
        pltpu.VMEM((REACH, 1, 4), jnp.int32),
        pltpu.VMEM((feats // 64, 256), F32),
        pltpu.VMEM((feats // 64, 256), F32),
        pltpu.VMEM((256, REACH * 128), BF),
        pltpu.VMEM((ny, nz, 2, rows, 128), BF),
        pltpu.VMEM((rows, 128), BF),
        pltpu.VMEM((REACH, rows, 128), BF),
        pltpu.VMEM((REACH, rows, 128), BF),
        pltpu.VMEM((nz, ny, rows, 128), F32),
        pltpu.VMEM((nz, ny, rows, 128), BF),
        pltpu.VMEM((nz, ny, rows, 128), BF),
        pltpu.VMEM((ny, nz, rows, 128), BF),
        pltpu.VMEM((ny, nz, rows, 128), BF),
        pltpu.VMEM((nz, rows, 128), BF),
        pltpu.VMEM((nz, rows, 128), BF),
        dma((10,)),
    ]
    for shape in (
        (REACH,),
        (nz,),
        (ny, nz),
        (ny, nz),
        (REACH,),
        (groups,),
        (ny, groups),
        (nz,),
        (1,),
    ):
        scratch += [dma(shape), dma(shape)]
    received = pl.pallas_call(
        functools.partial(kernel, sections, ny, nz),
        out_shape=jax.ShapeDtypeStruct((rows, 128), BF),
        in_specs=[pl.BlockSpec(memory_space=pl.ANY)] * 9,
        out_specs=pl.BlockSpec(memory_space=pltpu.VMEM),
        scratch_shapes=scratch,
        compiler_params=pltpu.CompilerParams(
            collective_id=0,
            has_side_effects=True,
            vmem_limit_bytes=67043328,
        ),
    )(
        tokens,
        norm_gain,
        gate_weight[0],
        up_weight[0],
        gate_mask[0].T,
        up_mask[0].T,
        down_weight[0],
        down_mask[0],
        slot_order,
    )
    return received[None]


def solution(mesh):
    return jax.shard_map(
        body,
        mesh=mesh,
        in_specs=(
            P(None, "tp"),
            P("section", None),
            P("section", None, "tp"),
            P("section", None, "tp"),
            P("section", None, "tp"),
            P("section", None, "tp"),
            P("section", "tp", None),
            P("section", "tp", None),
            P("section", "tp"),
        ),
        out_specs=P("section", None, "tp"),
        check_vma=False,
    )
```

```python
import functools

import jax
import jax.numpy as jnp
from jax import lax
from jax.experimental import pallas as pl
from jax.experimental.pallas import tpu as pltpu
from jax.sharding import PartitionSpec as P

MESH = pl.DeviceIdType.MESH
BF = jnp.bfloat16
F32 = jnp.float32
REACH = 4
GROUP = 2
ACROSS = (1,)
MOVE_FROM = 3


def tp_grid(count):
    ny = {64: 4, 32: 4, 16: 2, 8: 2}[count]
    return ny, count // (2 * ny)


def kernel(
    sections,
    ny,
    nz,
    tokens_h,
    gain_h,
    wg_h,
    wu_h,
    gm_h,
    um_h,
    wd_h,
    dm_h,
    so_h,
    out_ref,
    wg,
    wu,
    wd,
    wdp,
    gain,
    gm,
    um,
    dm,
    so_v,
    gme,
    ume,
    dme,
    perm,
    xbuf,
    xprev,
    hsend,
    hrecv,
    part,
    psend,
    precv,
    ysend,
    yrecv,
    zsend,
    zrecv,
    lsem,
    so_ss,
    so_rs,
    az_ss,
    az_rs,
    ay_ss,
    ay_rs,
    ap_ss,
    ap_rs,
    h_ss,
    h_rs,
    p_ss,
    p_rs,
    y_ss,
    y_rs,
    z_ss,
    z_rs,
    x_ss,
    x_rs,
    m_ss,
    m_rs,
):
    nt = ny * nz * 2
    rows = tokens_h.shape[0]
    feats = nt * 128
    groups = nz // GROUP
    s = lax.axis_index("section")
    t = lax.axis_index("tp")
    c = t % 2
    chip = t // 2
    z = chip % nz
    y = chip // nz
    s_next = (s + 1) % sections
    s_last = (s + sections - 1) % sections
    far = [nz // 2 + p // 2 if p % 2 == 0 else nz // 2 - 1 - p // 2 for p in range(nz)]
    near = far[::-1]
    y_far = [ny // 2] + [d for d in range(1, ny) if d != ny // 2]

    def pos(yy, zz):
        return (yy % ny) * nz + zz % nz

    def tp_of(yy, zz, cc):
        return pos(yy, zz) * 2 + cc

    partner = t + 1 - 2 * c

    def remote(src, dst, ss, rs, sec, tp):
        return pltpu.make_async_remote_copy(
            src_ref=src,
            dst_ref=dst,
            send_sem=ss,
            recv_sem=rs,
            device_id=(sec, tp),
            device_id_type=MESH,
        )

    loads = [
        pltpu.make_async_copy(src, dst, lsem.at[i])
        for i, (src, dst) in enumerate(
            [
                (so_h, so_v.at[0]),
                (gm_h, gm),
                (um_h, um),
                (dm_h, dm),
                (gain_h, gain),
                (wg_h, wg),
                (wu_h, wu),
                (wd_h, wd),
            ]
        )
    ]
    for one in loads:
        one.start()
    token_load = pltpu.make_async_copy(tokens_h, xbuf.at[0, 0, c], lsem.at[9])

    @pl.when(s == 0)
    def _():
        token_load.start()

    barrier = pltpu.get_barrier_semaphore()
    peers = [(s, partner)]
    peers += [(s, tp_of(y + d, z, c)) for d in range(1, ny)]
    peers += [(s, tp_of(y, z + d, c)) for d in range(1, nz)]
    peers += [(s, (t + d) % nt) for d in range(1, REACH)]
    peers += [(s, (t + nt - d) % nt) for d in range(1, REACH)]
    peers += [(s_next, tp_of(y, z + d, c)) for d in range(nz)]
    peers += [(s_last, tp_of(y, z + d, c)) for d in range(nz)]
    peers += [(s_next, tp_of(y + d, z, c)) for d in range(1, ny)]
    peers += [(s_last, tp_of(y + d, z, c)) for d in range(1, ny)]
    for peer in peers:
        pl.semaphore_signal(barrier, inc=1, device_id=peer, device_id_type=MESH)

    for one in loads[:5]:
        one.wait()

    spread_at = lax.broadcasted_iota(jnp.int32, (4, 256), 1) // 64
    spread_of = lax.broadcasted_iota(jnp.int32, (4, 256), 0)
    spread = jnp.where(spread_at == spread_of, 1.0, 0.0).astype(BF)
    for raw, wide in ((gm, gme), (um, ume)):
        wide[...] = lax.dot_general(
            raw[...].astype(BF),
            spread,
            (((0,), (0,)), ((), ())),
            preferred_element_type=F32,
        )

    def mask_up(weight, wide):
        @pl.loop(0, feats // 64, unroll=8)
        def _(i):
            at = pl.ds(pl.multiple_of(i * 64, 64), 64)
            row = jnp.broadcast_to(wide[pl.ds(i, 1), :], (16, 256)).astype(BF)
            block = weight[at, :].reshape(4, 16, 256) * row[None]
            weight[at, :] = block.reshape(64, 256)

    loads[5].wait()
    mask_up(wg, gme)
    loads[6].wait()
    mask_up(wu, ume)

    down_bits = dm[...].astype(BF)
    entries = feats // 64
    pick_row = lax.broadcasted_iota(jnp.int32, (entries, entries), 0)
    pick_lane = lax.broadcasted_iota(jnp.int32, (entries, entries), 1)
    row_is = lax.broadcasted_iota(jnp.int32, (4, entries), 0)
    lane_is = lax.broadcasted_iota(jnp.int32, (4, entries), 1)
    turned = jnp.zeros((4, entries), F32)
    for q in range(4):
        pick = jnp.where(pick_row == pick_lane // 4 * 4 + q, 1.0, 0.0).astype(BF)
        found = jnp.dot(down_bits, pick, preferred_element_type=F32)
        found = jnp.where(row_is == lane_is % 4, found, 0.0)
        found = jnp.sum(found, axis=0, keepdims=True)
        turned = turned + jnp.where(row_is == q, found, 0.0)
    dme[...] = lax.dot_general(
        turned.astype(BF),
        spread,
        (((0,), (0,)), ((), ())),
        preferred_element_type=F32,
    )
    sort_row = lax.broadcasted_iota(jnp.int32, (256, 256), 0)
    sort_lane = lax.broadcasted_iota(jnp.int32, (256, 256), 1)
    sender = (so_v[0] // 4 + nt - t) % nt
    sender_of = jnp.zeros((1, 256), jnp.int32)
    for k in range(REACH):
        sender_of = jnp.where(
            sort_lane[:1] // 64 == k, sender[:, k : k + 1], sender_of
        )
    same = (sort_row // 64 == sender_of) & (sort_row % 64 == sort_lane % 64)
    sort = jnp.where(same, 1.0, 0.0).astype(BF)

    def mask_down(first, last):
        @pl.loop(first, last, unroll=2)
        def _(i):
            cols = pl.ds(pl.multiple_of(i * 256, 256), 256)
            blocks = []
            for k in range(REACH):
                row = dme[pl.ds(4 * i + k, 1), :]
                row = jnp.broadcast_to(row, (16, 256)).astype(BF)
                block = wd[k * 64 : (k + 1) * 64, cols]
                block = block.reshape(4, 16, 256) * row[None]
                blocks.append(block.reshape(64, 256))
            wdp[0, :, cols] = jnp.dot(
                sort, jnp.concatenate(blocks, axis=0), preferred_element_type=F32
            ).astype(BF)

    tiles_down = feats // 256
    early, middle = tiles_down * 3 // 16 * 2, tiles_down * 5 // 16 * 2
    loads[7].wait()
    mask_down(0, early)

    pl.semaphore_wait(barrier, len(peers))

    own = xbuf.at[0, 0, c]

    def z_gather(d):
        return remote(
            own, xbuf.at[0, d, c], az_ss.at[d], az_rs.at[d], s, tp_of(y, z + d, c)
        )

    def y_gather(dy, d):
        return remote(
            xbuf.at[0, d, c],
            xbuf.at[dy, d, c],
            ay_ss.at[dy, d],
            ay_rs.at[dy, d],
            s,
            tp_of(y + dy, z, c),
        )

    def p_gather(dy, d):
        return remote(
            xbuf.at[dy, d, c],
            xbuf.at[dy, d, c],
            ap_ss.at[dy, d],
            ap_rs.at[dy, d],
            s,
            partner,
        )

    keep_copy = remote(own, xprev, x_ss.at[0], x_rs.at[0], s_next, t)

    def z_scatter(p):
        return remote(
            zsend.at[p],
            zrecv.at[p],
            z_ss.at[p],
            z_rs.at[p],
            s if p // GROUP in ACROSS else s_next,
            tp_of(y, z + far[p], c),
        )

    def y_scatter(dy, g):
        some = pl.ds(g * GROUP, GROUP)
        return remote(
            ysend.at[dy, some],
            yrecv.at[dy, some],
            y_ss.at[dy, g],
            y_rs.at[dy, g],
            s_next if g in ACROSS else s,
            tp_of(y + dy, z, c),
        )

    def send_own():
        for d in far[:-1]:
            z_gather(d).start()
        for dy in y_far:
            y_gather(dy, 0).start()
        p_gather(0, 0).start()
        keep_copy.start()

    def arrive():
        for g in ACROSS:
            for dy in range(ny):
                y_scatter(dy, g).wait_recv()
            for p in range(g * GROUP, (g + 1) * GROUP):
                total = yrecv[0, p].astype(F32)
                for dy in range(1, ny):
                    total = total + yrecv[dy, p].astype(F32)
                zsend[p] = total.astype(BF)
                z_scatter(p).start()
        keep_copy.wait_recv()
        total = xprev[...].astype(F32)
        for p in range(nz):
            z_scatter(p).wait_recv()
            total = total + zrecv[p].astype(F32)
        return total.astype(BF)

    @pl.when(s == 0)
    def _():
        token_load.wait()
        send_own()

    so_copies = [
        remote(so_v.at[0], so_v.at[j], so_ss.at[j], so_rs.at[j], s, (t + j) % nt)
        for j in range(1, REACH)
    ]
    for one in so_copies:
        one.start()

    mask_down(early, middle)

    for one in so_copies:
        one.wait_recv()
    row_of = lax.broadcasted_iota(jnp.int32, (256, 128), 0)
    lane_of = lax.broadcasted_iota(jnp.int32, (256, 128), 1)
    for j in range(REACH):
        order = so_v[j]
        mine = jnp.sum(
            jnp.where(order // 4 == t, order % 4, 0), axis=1, keepdims=True
        )
        hit = (row_of == mine * 64 + lane_of % 64) & (lane_of // 64 == j % 2)
        perm[:, j * 128 : (j + 1) * 128] = jnp.where(hit, 1.0, 0.0).astype(BF)

    def move(j):
        block = pl.ds(j * 64, 64)
        return remote(
            wdp.at[0, block],
            wdp.at[1, block],
            m_ss.at[j],
            m_rs.at[j],
            s,
            (t + j) % nt,
        )

    moved = jnp.where(s >= MOVE_FROM, 1, 0)

    @pl.when(s > 0)
    def _():
        mask_down(middle, tiles_down)

    @pl.when(s >= MOVE_FROM)
    def _():
        for j in range(1, REACH):
            move(j).start()
        stay = pltpu.make_async_copy(
            wdp.at[0, pl.ds(0, 64)], wdp.at[1, pl.ds(0, 64)], m_rs.at[0]
        )
        stay.start()
        for j in range(1, REACH):
            move(j).wait()
        stay.wait()

    @pl.when(s > 0)
    def _():
        rows_in = arrive()
        xbuf[0, 0, c] = rows_in
        out_ref[...] = rows_in
        send_own()

    def block_product(d, state):
        gate, upper, squares = state
        for dy in range(ny):
            at = pos(y + ny - dy, z + nz - d)
            wide = jnp.concatenate(
                [xbuf[dy, d, 0], xbuf[dy, d, 1]], axis=1
            ).astype(F32)
            squares = squares + wide * wide
            where = pl.ds(pl.multiple_of(at * 256, 256), 256)
            left = (wide * gain[:, where]).astype(BF)
            gate = gate + jnp.dot(left, wg[where, :], preferred_element_type=F32)
            upper = upper + jnp.dot(left, wu[where, :], preferred_element_type=F32)
        return gate, upper, squares

    state = tuple(jnp.zeros((rows, 256), F32) for _ in range(3))
    for d in near[1:]:
        z_gather(d).wait_recv()
        for dy in y_far:
            y_gather(dy, d).start()
        p_gather(0, d).start()

    @pl.when(s == 0)
    def _():
        mask_down(middle, tiles_down)

    for step in range(nz + 1):
        if step < nz:
            d = near[step]
            for dy in y_far[::-1]:
                y_gather(dy, d).wait_recv()
                p_gather(dy, d).start()
        if step >= 1:
            d = near[step - 1]
            for dy in range(ny):
                remote(
                    xbuf.at[dy, d, c],
                    xbuf.at[dy, d, 1 - c],
                    ap_ss.at[dy, d],
                    ap_rs.at[dy, d],
                    s,
                    partner,
                ).wait_recv()
            state = block_product(d, state)
    gate, upper, squares = state
    scale = lax.rsqrt(jnp.sum(squares, axis=1, keepdims=True) / feats + 1e-05)
    gate = gate * scale
    hidden = (gate / (1.0 + jnp.exp(-gate)) * (upper * scale)).astype(BF)
    routed = jnp.dot(hidden, perm[...], preferred_element_type=F32).astype(BF)

    def hand_over(j):
        return remote(
            hsend.at[j], hrecv.at[j], h_ss.at[j], h_rs.at[j], s, (t + nt - j) % nt
        )

    @pl.when(s < MOVE_FROM)
    def _():
        for j in range(REACH - 1, 0, -1):
            hsend[j] = routed[:, j * 128 : (j + 1) * 128]
            hand_over(j).start()
        for j in range(1, REACH):
            hand_over(j).wait()

    @pl.when(s >= MOVE_FROM)
    def _():
        for j in range(1, REACH):
            hrecv[j] = routed[:, j * 128 : (j + 1) * 128]

    tiles = jnp.concatenate(
        [routed[:, :128] + hrecv[1], hrecv[2] + hrecv[3]], axis=1
    )

    def p_scatter(g):
        some = pl.ds(g * GROUP, GROUP)
        return remote(
            psend.at[some], precv.at[some], p_ss.at[g], p_rs.at[g], s, partner
        )

    for g in range(groups):
        for p in range(g * GROUP, (g + 1) * GROUP):
            for dy in range(ny):
                at = pos(y + dy, z + far[p])
                cols = pl.ds(pl.multiple_of(at * 256, 256), 256)
                both = jnp.dot(tiles, wdp[moved, :, cols], preferred_element_type=F32)
                low, high = both[:, :128], both[:, 128:]
                part[p, dy] = jnp.where(c == 0, low, high)
                psend[p, dy] = jnp.where(c == 0, high, low).astype(BF)
        p_scatter(g).start()
    for g in range(groups):
        p_scatter(g).wait_recv()
        for dy in y_far + ([0] if g in ACROSS else []):
            for p in range(g * GROUP, (g + 1) * GROUP):
                ysend[dy, p] = (part[p, dy] + precv[p, dy].astype(F32)).astype(BF)
            y_scatter(dy, g).start()
    for g in range(groups):
        if g in ACROSS:
            continue
        for dy in y_far[::-1]:
            y_scatter(dy, g).wait_recv()
        for p in range(g * GROUP, (g + 1) * GROUP):
            total = part[p, 0] + precv[p, 0].astype(F32)
            for dy in range(1, ny):
                total = total + yrecv[dy, p].astype(F32)
            zsend[p] = total.astype(BF)
            z_scatter(p).start()

    @pl.when(s == 0)
    def _():
        out_ref[...] = arrive()

    for one in so_copies:
        one.wait_send()
    keep_copy.wait_send()
    for d in range(1, nz):
        z_gather(d).wait_send()
    for d in range(nz):
        for dy in range(1, ny):
            y_gather(dy, d).wait_send()
        for dy in range(ny):
            p_gather(dy, d).wait_send()
        z_scatter(d).wait_send()
    for g in range(groups):
        p_scatter(g).wait_send()
        for dy in range(0 if g in ACROSS else 1, ny):
            y_scatter(dy, g).wait_send()


def body(
    tokens,
    norm_gain,
    gate_weight,
    up_weight,
    gate_mask,
    up_mask,
    down_weight,
    down_mask,
    slot_order,
):
    sections = lax.axis_size("section")
    nt = lax.axis_size("tp")
    ny, nz = tp_grid(nt)
    rows = tokens.shape[0]
    feats = nt * 128
    groups = nz // GROUP
    dma = pltpu.SemaphoreType.DMA
    scratch = [
        pltpu.VMEM((feats, 256), BF),
        pltpu.VMEM((feats, 256), BF),
        pltpu.VMEM((256, feats), BF),
        pltpu.VMEM((2, 256, feats), BF),
        pltpu.VMEM((1, feats), F32),
        pltpu.VMEM((4, feats // 64), jnp.int32),
        pltpu.VMEM((4, feats // 64), jnp.int32),
        pltpu.VMEM((4, feats // 64), jnp.int32),
        pltpu.VMEM((REACH, 1, 4), jnp.int32),
        pltpu.VMEM((feats // 64, 256), F32),
        pltpu.VMEM((feats // 64, 256), F32),
        pltpu.VMEM((feats // 64, 256), F32),
        pltpu.VMEM((256, REACH * 128), BF),
        pltpu.VMEM((ny, nz, 2, rows, 128), BF),
        pltpu.VMEM((rows, 128), BF),
        pltpu.VMEM((REACH, rows, 128), BF),
        pltpu.VMEM((REACH, rows, 128), BF),
        pltpu.VMEM((nz, ny, rows, 128), F32),
        pltpu.VMEM((nz, ny, rows, 128), BF),
        pltpu.VMEM((nz, ny, rows, 128), BF),
        pltpu.VMEM((ny, nz, rows, 128), BF),
        pltpu.VMEM((ny, nz, rows, 128), BF),
        pltpu.VMEM((nz, rows, 128), BF),
        pltpu.VMEM((nz, rows, 128), BF),
        dma((10,)),
    ]
    for shape in (
        (REACH,),
        (nz,),
        (ny, nz),
        (ny, nz),
        (REACH,),
        (groups,),
        (ny, groups),
        (nz,),
        (1,),
        (REACH,),
    ):
        scratch += [dma(shape), dma(shape)]
    received = pl.pallas_call(
        functools.partial(kernel, sections, ny, nz),
        out_shape=jax.ShapeDtypeStruct((rows, 128), BF),
        in_specs=[pl.BlockSpec(memory_space=pl.ANY)] * 9,
        out_specs=pl.BlockSpec(memory_space=pltpu.VMEM),
        scratch_shapes=scratch,
        compiler_params=pltpu.CompilerParams(
            collective_id=0,
            has_side_effects=True,
            vmem_limit_bytes=67043328,
        ),
    )(
        tokens,
        norm_gain,
        gate_weight[0],
        up_weight[0],
        gate_mask[0].T,
        up_mask[0].T,
        down_weight[0],
        down_mask[0],
        slot_order,
    )
    return received[None]


def solution(mesh):
    return jax.shard_map(
        body,
        mesh=mesh,
        in_specs=(
            P(None, "tp"),
            P("section", None),
            P("section", None, "tp"),
            P("section", None, "tp"),
            P("section", None, "tp"),
            P("section", None, "tp"),
            P("section", "tp", None),
            P("section", "tp", None),
            P("section", "tp"),
        ),
        out_specs=P("section", None, "tp"),
        check_vma=False,
    )
```

```python
import functools

import jax
import jax.numpy as jnp
from jax import lax
from jax.experimental import pallas as pl
from jax.experimental.pallas import tpu as pltpu
from jax.sharding import PartitionSpec as P

MESH = pl.DeviceIdType.MESH
BF = jnp.bfloat16
F32 = jnp.float32
REACH = 4
GROUP = 2
ACROSS = (1,)
MOVE_FROM = 3


def tp_grid(count):
    ny = {64: 4, 32: 4, 16: 2, 8: 2}[count]
    return ny, count // (2 * ny)


def kernel(
    sections,
    ny,
    nz,
    tokens_h,
    gain_h,
    wg_h,
    wu_h,
    gm_h,
    um_h,
    wd_h,
    dm_h,
    so_h,
    out_ref,
    wg,
    wu,
    wd,
    wdp,
    gain,
    gm,
    um,
    dm,
    so_v,
    gme,
    ume,
    dme,
    perm,
    xbuf,
    xprev,
    hsend,
    hrecv,
    part,
    psend,
    precv,
    ysend,
    yrecv,
    zsend,
    zrecv,
    lsem,
    so_ss,
    so_rs,
    az_ss,
    az_rs,
    ay_ss,
    ay_rs,
    ap_ss,
    ap_rs,
    h_ss,
    h_rs,
    p_ss,
    p_rs,
    y_ss,
    y_rs,
    z_ss,
    z_rs,
    x_ss,
    x_rs,
    m_ss,
    m_rs,
):
    nt = ny * nz * 2
    rows = tokens_h.shape[0]
    feats = nt * 128
    groups = nz // GROUP
    s = lax.axis_index("section")
    t = lax.axis_index("tp")
    c = t % 2
    chip = t // 2
    z = chip % nz
    y = chip // nz
    s_next = (s + 1) % sections
    s_last = (s + sections - 1) % sections
    far = [nz // 2 + p // 2 if p % 2 == 0 else nz // 2 - 1 - p // 2 for p in range(nz)]
    near = far[::-1]
    y_far = [ny // 2] + [d for d in range(1, ny) if d != ny // 2]

    def pos(yy, zz):
        return (yy % ny) * nz + zz % nz

    def tp_of(yy, zz, cc):
        return pos(yy, zz) * 2 + cc

    partner = t + 1 - 2 * c

    def remote(src, dst, ss, rs, sec, tp):
        return pltpu.make_async_remote_copy(
            src_ref=src,
            dst_ref=dst,
            send_sem=ss,
            recv_sem=rs,
            device_id=(sec, tp),
            device_id_type=MESH,
        )

    loads = [
        pltpu.make_async_copy(src, dst, lsem.at[i])
        for i, (src, dst) in enumerate(
            [
                (so_h, so_v.at[0]),
                (gm_h, gm),
                (um_h, um),
                (dm_h, dm),
                (gain_h, gain),
                (wg_h, wg),
                (wu_h, wu),
                (wd_h, wd),
            ]
        )
    ]
    for one in loads:
        one.start()
    token_load = pltpu.make_async_copy(tokens_h, xbuf.at[0, 0, c], lsem.at[9])

    @pl.when(s == 0)
    def _():
        token_load.start()

    barrier = pltpu.get_barrier_semaphore()
    peers = [(s, partner)]
    peers += [(s, tp_of(y + d, z, c)) for d in range(1, ny)]
    peers += [(s, tp_of(y, z + d, c)) for d in range(1, nz)]
    peers += [(s, (t + d) % nt) for d in range(1, REACH)]
    peers += [(s, (t + nt - d) % nt) for d in range(1, REACH)]
    peers += [(s_next, tp_of(y, z + d, c)) for d in range(nz)]
    peers += [(s_last, tp_of(y, z + d, c)) for d in range(nz)]
    peers += [(s_next, tp_of(y + d, z, c)) for d in range(1, ny)]
    peers += [(s_last, tp_of(y + d, z, c)) for d in range(1, ny)]
    for peer in peers:
        pl.semaphore_signal(barrier, inc=1, device_id=peer, device_id_type=MESH)

    for one in loads[:5]:
        one.wait()

    spread_at = lax.broadcasted_iota(jnp.int32, (4, 256), 1) // 64
    spread_of = lax.broadcasted_iota(jnp.int32, (4, 256), 0)
    spread = jnp.where(spread_at == spread_of, 1.0, 0.0).astype(BF)
    for raw, wide in ((gm, gme), (um, ume)):
        wide[...] = lax.dot_general(
            raw[...].astype(BF),
            spread,
            (((0,), (0,)), ((), ())),
            preferred_element_type=F32,
        )

    def mask_up(weight, wide):
        @pl.loop(0, feats // 64, unroll=8)
        def _(i):
            at = pl.ds(pl.multiple_of(i * 64, 64), 64)
            row = jnp.broadcast_to(wide[pl.ds(i, 1), :], (16, 256)).astype(BF)
            block = weight[at, :].reshape(4, 16, 256) * row[None]
            weight[at, :] = block.reshape(64, 256)

    loads[5].wait()
    mask_up(wg, gme)
    loads[6].wait()
    mask_up(wu, ume)

    down_bits = dm[...].astype(BF)
    entries = feats // 64
    pick_row = lax.broadcasted_iota(jnp.int32, (entries, entries), 0)
    pick_lane = lax.broadcasted_iota(jnp.int32, (entries, entries), 1)
    row_is = lax.broadcasted_iota(jnp.int32, (4, entries), 0)
    lane_is = lax.broadcasted_iota(jnp.int32, (4, entries), 1)
    turned = jnp.zeros((4, entries), F32)
    for q in range(4):
        pick = jnp.where(pick_row == pick_lane // 4 * 4 + q, 1.0, 0.0).astype(BF)
        found = jnp.dot(down_bits, pick, preferred_element_type=F32)
        found = jnp.where(row_is == lane_is % 4, found, 0.0)
        found = jnp.sum(found, axis=0, keepdims=True)
        turned = turned + jnp.where(row_is == q, found, 0.0)
    dme[...] = lax.dot_general(
        turned.astype(BF),
        spread,
        (((0,), (0,)), ((), ())),
        preferred_element_type=F32,
    )
    sort_row = lax.broadcasted_iota(jnp.int32, (256, 256), 0)
    sort_lane = lax.broadcasted_iota(jnp.int32, (256, 256), 1)
    sender = (so_v[0] // 4 + nt - t) % nt
    sender_of = jnp.zeros((1, 256), jnp.int32)
    for k in range(REACH):
        sender_of = jnp.where(
            sort_lane[:1] // 64 == k, sender[:, k : k + 1], sender_of
        )
    same = (sort_row // 64 == sender_of) & (sort_row % 64 == sort_lane % 64)
    sort = jnp.where(same, 1.0, 0.0).astype(BF)

    def mask_down(first, last):
        @pl.loop(first, last, unroll=4)
        def _(i):
            cols = pl.ds(pl.multiple_of(i * 256, 256), 256)
            blocks = []
            for k in range(REACH):
                row = dme[pl.ds(4 * i + k, 1), :]
                row = jnp.broadcast_to(row, (16, 256)).astype(BF)
                block = wd[k * 64 : (k + 1) * 64, cols]
                block = block.reshape(4, 16, 256) * row[None]
                blocks.append(block.reshape(64, 256))
            wdp[0, :, cols] = jnp.dot(
                sort, jnp.concatenate(blocks, axis=0), preferred_element_type=F32
            ).astype(BF)

    tiles_down = feats // 256
    early, middle = tiles_down // 4, tiles_down // 2
    loads[7].wait()
    mask_down(0, early)

    pl.semaphore_wait(barrier, len(peers))

    own = xbuf.at[0, 0, c]

    def z_gather(d):
        return remote(
            own, xbuf.at[0, d, c], az_ss.at[d], az_rs.at[d], s, tp_of(y, z + d, c)
        )

    def y_gather(dy, d):
        return remote(
            xbuf.at[0, d, c],
            xbuf.at[dy, d, c],
            ay_ss.at[dy, d],
            ay_rs.at[dy, d],
            s,
            tp_of(y + dy, z, c),
        )

    def p_gather(dy, d):
        return remote(
            xbuf.at[dy, d, c],
            xbuf.at[dy, d, c],
            ap_ss.at[dy, d],
            ap_rs.at[dy, d],
            s,
            partner,
        )

    keep_copy = remote(own, xprev, x_ss.at[0], x_rs.at[0], s_next, t)

    def z_scatter(p):
        return remote(
            zsend.at[p],
            zrecv.at[p],
            z_ss.at[p],
            z_rs.at[p],
            s if p // GROUP in ACROSS else s_next,
            tp_of(y, z + far[p], c),
        )

    def y_scatter(dy, g):
        some = pl.ds(g * GROUP, GROUP)
        return remote(
            ysend.at[dy, some],
            yrecv.at[dy, some],
            y_ss.at[dy, g],
            y_rs.at[dy, g],
            s_next if g in ACROSS else s,
            tp_of(y + dy, z, c),
        )

    def send_own():
        for d in far[:-1]:
            z_gather(d).start()
        for dy in y_far:
            y_gather(dy, 0).start()
        p_gather(0, 0).start()
        keep_copy.start()

    def arrive():
        for g in ACROSS:
            for dy in range(ny):
                y_scatter(dy, g).wait_recv()
            for p in range(g * GROUP, (g + 1) * GROUP):
                total = yrecv[0, p].astype(F32)
                for dy in range(1, ny):
                    total = total + yrecv[dy, p].astype(F32)
                zsend[p] = total.astype(BF)
                z_scatter(p).start()
        keep_copy.wait_recv()
        total = xprev[...].astype(F32)
        for p in range(nz):
            z_scatter(p).wait_recv()
            total = total + zrecv[p].astype(F32)
        return total.astype(BF)

    @pl.when(s == 0)
    def _():
        token_load.wait()
        send_own()

    so_copies = [
        remote(so_v.at[0], so_v.at[j], so_ss.at[j], so_rs.at[j], s, (t + j) % nt)
        for j in range(1, REACH)
    ]
    for one in so_copies:
        one.start()

    mask_down(early, middle)

    for one in so_copies:
        one.wait_recv()
    row_of = lax.broadcasted_iota(jnp.int32, (256, 128), 0)
    lane_of = lax.broadcasted_iota(jnp.int32, (256, 128), 1)
    for j in range(REACH):
        order = so_v[j]
        mine = jnp.sum(
            jnp.where(order // 4 == t, order % 4, 0), axis=1, keepdims=True
        )
        hit = (row_of == mine * 64 + lane_of % 64) & (lane_of // 64 == j % 2)
        perm[:, j * 128 : (j + 1) * 128] = jnp.where(hit, 1.0, 0.0).astype(BF)

    def move(j):
        block = pl.ds(j * 64, 64)
        return remote(
            wdp.at[0, block],
            wdp.at[1, block],
            m_ss.at[j],
            m_rs.at[j],
            s,
            (t + j) % nt,
        )

    moved = jnp.where(s >= MOVE_FROM, 1, 0)

    @pl.when(s > 0)
    def _():
        mask_down(middle, tiles_down)

    @pl.when(s >= MOVE_FROM)
    def _():
        for j in range(1, REACH):
            move(j).start()
        stay = pltpu.make_async_copy(
            wdp.at[0, pl.ds(0, 64)], wdp.at[1, pl.ds(0, 64)], m_rs.at[0]
        )
        stay.start()
        for j in range(1, REACH):
            move(j).wait()
        stay.wait()

    @pl.when(s > 0)
    def _():
        rows_in = arrive()
        xbuf[0, 0, c] = rows_in
        out_ref[...] = rows_in
        send_own()

    def block_product(d, state):
        gate, upper, squares = state
        for dy in range(ny):
            at = pos(y + ny - dy, z + nz - d)
            wide = jnp.concatenate(
                [xbuf[dy, d, 0], xbuf[dy, d, 1]], axis=1
            ).astype(F32)
            squares = squares + wide * wide
            where = pl.ds(pl.multiple_of(at * 256, 256), 256)
            left = (wide * gain[:, where]).astype(BF)
            gate = gate + jnp.dot(left, wg[where, :], preferred_element_type=F32)
            upper = upper + jnp.dot(left, wu[where, :], preferred_element_type=F32)
        return gate, upper, squares

    state = tuple(jnp.zeros((rows, 256), F32) for _ in range(3))
    for d in near[1:]:
        z_gather(d).wait_recv()
        for dy in y_far:
            y_gather(dy, d).start()
        p_gather(0, d).start()

    @pl.when(s == 0)
    def _():
        mask_down(middle, tiles_down)

    for step in range(nz + 1):
        if step < nz:
            d = near[step]
            for dy in y_far[::-1]:
                y_gather(dy, d).wait_recv()
                p_gather(dy, d).start()
        if step >= 1:
            d = near[step - 1]
            for dy in range(ny):
                remote(
                    xbuf.at[dy, d, c],
                    xbuf.at[dy, d, 1 - c],
                    ap_ss.at[dy, d],
                    ap_rs.at[dy, d],
                    s,
                    partner,
                ).wait_recv()
            state = block_product(d, state)
    gate, upper, squares = state
    scale = lax.rsqrt(jnp.sum(squares, axis=1, keepdims=True) / feats + 1e-05)
    gate = gate * scale
    hidden = (gate / (1.0 + jnp.exp(-gate)) * (upper * scale)).astype(BF)
    routed = jnp.dot(hidden, perm[...], preferred_element_type=F32).astype(BF)

    def hand_over(j):
        return remote(
            hsend.at[j], hrecv.at[j], h_ss.at[j], h_rs.at[j], s, (t + nt - j) % nt
        )

    @pl.when(s < MOVE_FROM)
    def _():
        for j in range(REACH - 1, 0, -1):
            hsend[j] = routed[:, j * 128 : (j + 1) * 128]
            hand_over(j).start()
        for j in range(1, REACH):
            hand_over(j).wait()

    @pl.when(s >= MOVE_FROM)
    def _():
        for j in range(1, REACH):
            hrecv[j] = routed[:, j * 128 : (j + 1) * 128]

    tiles = jnp.concatenate(
        [routed[:, :128] + hrecv[1], hrecv[2] + hrecv[3]], axis=1
    )

    def p_scatter(g):
        some = pl.ds(g * GROUP, GROUP)
        return remote(
            psend.at[some], precv.at[some], p_ss.at[g], p_rs.at[g], s, partner
        )

    for g in range(groups):
        for p in range(g * GROUP, (g + 1) * GROUP):
            for dy in range(ny):
                at = pos(y + dy, z + far[p])
                cols = pl.ds(pl.multiple_of(at * 256, 256), 256)
                both = jnp.dot(tiles, wdp[moved, :, cols], preferred_element_type=F32)
                low, high = both[:, :128], both[:, 128:]
                part[p, dy] = jnp.where(c == 0, low, high)
                psend[p, dy] = jnp.where(c == 0, high, low).astype(BF)
        p_scatter(g).start()
    for g in range(groups):
        p_scatter(g).wait_recv()
        for dy in y_far + ([0] if g in ACROSS else []):
            for p in range(g * GROUP, (g + 1) * GROUP):
                ysend[dy, p] = (part[p, dy] + precv[p, dy].astype(F32)).astype(BF)
            y_scatter(dy, g).start()
    for g in range(groups):
        if g in ACROSS:
            continue
        for dy in y_far[::-1]:
            y_scatter(dy, g).wait_recv()
        for p in range(g * GROUP, (g + 1) * GROUP):
            total = part[p, 0] + precv[p, 0].astype(F32)
            for dy in range(1, ny):
                total = total + yrecv[dy, p].astype(F32)
            zsend[p] = total.astype(BF)
            z_scatter(p).start()

    @pl.when(s == 0)
    def _():
        out_ref[...] = arrive()

    for one in so_copies:
        one.wait_send()
    keep_copy.wait_send()
    for d in range(1, nz):
        z_gather(d).wait_send()
    for d in range(nz):
        for dy in range(1, ny):
            y_gather(dy, d).wait_send()
        for dy in range(ny):
            p_gather(dy, d).wait_send()
        z_scatter(d).wait_send()
    for g in range(groups):
        p_scatter(g).wait_send()
        for dy in range(0 if g in ACROSS else 1, ny):
            y_scatter(dy, g).wait_send()


def body(
    tokens,
    norm_gain,
    gate_weight,
    up_weight,
    gate_mask,
    up_mask,
    down_weight,
    down_mask,
    slot_order,
):
    sections = lax.axis_size("section")
    nt = lax.axis_size("tp")
    ny, nz = tp_grid(nt)
    rows = tokens.shape[0]
    feats = nt * 128
    groups = nz // GROUP
    dma = pltpu.SemaphoreType.DMA
    scratch = [
        pltpu.VMEM((feats, 256), BF),
        pltpu.VMEM((feats, 256), BF),
        pltpu.VMEM((256, feats), BF),
        pltpu.VMEM((2, 256, feats), BF),
        pltpu.VMEM((1, feats), F32),
        pltpu.VMEM((4, feats // 64), jnp.int32),
        pltpu.VMEM((4, feats // 64), jnp.int32),
        pltpu.VMEM((4, feats // 64), jnp.int32),
        pltpu.VMEM((REACH, 1, 4), jnp.int32),
        pltpu.VMEM((feats // 64, 256), F32),
        pltpu.VMEM((feats // 64, 256), F32),
        pltpu.VMEM((feats // 64, 256), F32),
        pltpu.VMEM((256, REACH * 128), BF),
        pltpu.VMEM((ny, nz, 2, rows, 128), BF),
        pltpu.VMEM((rows, 128), BF),
        pltpu.VMEM((REACH, rows, 128), BF),
        pltpu.VMEM((REACH, rows, 128), BF),
        pltpu.VMEM((nz, ny, rows, 128), F32),
        pltpu.VMEM((nz, ny, rows, 128), BF),
        pltpu.VMEM((nz, ny, rows, 128), BF),
        pltpu.VMEM((ny, nz, rows, 128), BF),
        pltpu.VMEM((ny, nz, rows, 128), BF),
        pltpu.VMEM((nz, rows, 128), BF),
        pltpu.VMEM((nz, rows, 128), BF),
        dma((10,)),
    ]
    for shape in (
        (REACH,),
        (nz,),
        (ny, nz),
        (ny, nz),
        (REACH,),
        (groups,),
        (ny, groups),
        (nz,),
        (1,),
        (REACH,),
    ):
        scratch += [dma(shape), dma(shape)]
    received = pl.pallas_call(
        functools.partial(kernel, sections, ny, nz),
        out_shape=jax.ShapeDtypeStruct((rows, 128), BF),
        in_specs=[pl.BlockSpec(memory_space=pl.ANY)] * 9,
        out_specs=pl.BlockSpec(memory_space=pltpu.VMEM),
        scratch_shapes=scratch,
        compiler_params=pltpu.CompilerParams(
            collective_id=0,
            has_side_effects=True,
            vmem_limit_bytes=67043328,
        ),
    )(
        tokens,
        norm_gain,
        gate_weight[0],
        up_weight[0],
        gate_mask[0].T,
        up_mask[0].T,
        down_weight[0],
        down_mask[0],
        slot_order,
    )
    return received[None]


def solution(mesh):
    return jax.shard_map(
        body,
        mesh=mesh,
        in_specs=(
            P(None, "tp"),
            P("section", None),
            P("section", None, "tp"),
            P("section", None, "tp"),
            P("section", None, "tp"),
            P("section", None, "tp"),
            P("section", "tp", None),
            P("section", "tp", None),
            P("section", "tp"),
        ),
        out_specs=P("section", None, "tp"),
        check_vma=False,
    )
```

```python
import functools

import jax
import jax.numpy as jnp
from jax import lax
from jax.experimental import pallas as pl
from jax.experimental.pallas import tpu as pltpu
from jax.sharding import PartitionSpec as P

MESH = pl.DeviceIdType.MESH
BF = jnp.bfloat16
F32 = jnp.float32
REACH = 4
GROUP = 2
LAG = 2
ACROSS = (1,)
MOVE_FROM = 3


def tp_grid(count):
    ny = {64: 4, 32: 4, 16: 2, 8: 2}[count]
    return ny, count // (2 * ny)


def kernel(
    sections,
    ny,
    nz,
    tokens_h,
    gain_h,
    wg_h,
    wu_h,
    gm_h,
    um_h,
    wd_h,
    dm_h,
    so_h,
    out_ref,
    wg,
    wu,
    wd,
    wdp,
    gain,
    gm,
    um,
    dm,
    so_v,
    gme,
    ume,
    dme,
    perm,
    xbuf,
    xprev,
    hsend,
    hrecv,
    part,
    psend,
    precv,
    ysend,
    yrecv,
    zsend,
    zrecv,
    lsem,
    so_ss,
    so_rs,
    az_ss,
    az_rs,
    ay_ss,
    ay_rs,
    ap_ss,
    ap_rs,
    h_ss,
    h_rs,
    p_ss,
    p_rs,
    y_ss,
    y_rs,
    z_ss,
    z_rs,
    x_ss,
    x_rs,
    m_ss,
    m_rs,
):
    nt = ny * nz * 2
    rows = tokens_h.shape[0]
    feats = nt * 128
    groups = nz // GROUP
    s = lax.axis_index("section")
    t = lax.axis_index("tp")
    c = t % 2
    chip = t // 2
    z = chip % nz
    y = chip // nz
    s_next = (s + 1) % sections
    s_last = (s + sections - 1) % sections
    far = [nz // 2 + p // 2 if p % 2 == 0 else nz // 2 - 1 - p // 2 for p in range(nz)]
    near = far[::-1]
    y_far = [ny // 2] + [d for d in range(1, ny) if d != ny // 2]

    def pos(yy, zz):
        return (yy % ny) * nz + zz % nz

    def tp_of(yy, zz, cc):
        return pos(yy, zz) * 2 + cc

    partner = t + 1 - 2 * c

    def remote(src, dst, ss, rs, sec, tp):
        return pltpu.make_async_remote_copy(
            src_ref=src,
            dst_ref=dst,
            send_sem=ss,
            recv_sem=rs,
            device_id=(sec, tp),
            device_id_type=MESH,
        )

    loads = [
        pltpu.make_async_copy(src, dst, lsem.at[i])
        for i, (src, dst) in enumerate(
            [
                (so_h, so_v.at[0]),
                (gm_h, gm),
                (um_h, um),
                (dm_h, dm),
                (gain_h, gain),
                (wg_h, wg),
                (wu_h, wu),
                (wd_h, wd),
            ]
        )
    ]
    for one in loads:
        one.start()
    token_load = pltpu.make_async_copy(tokens_h, xbuf.at[0, 0, c], lsem.at[9])

    @pl.when(s == 0)
    def _():
        token_load.start()

    barrier = pltpu.get_barrier_semaphore()
    peers = [(s, partner)]
    peers += [(s, tp_of(y + d, z, c)) for d in range(1, ny)]
    peers += [(s, tp_of(y, z + d, c)) for d in range(1, nz)]
    peers += [(s, (t + d) % nt) for d in range(1, REACH)]
    peers += [(s, (t + nt - d) % nt) for d in range(1, REACH)]
    peers += [(s_next, tp_of(y, z + d, c)) for d in range(nz)]
    peers += [(s_last, tp_of(y, z + d, c)) for d in range(nz)]
    peers += [(s_next, tp_of(y + d, z, c)) for d in range(1, ny)]
    peers += [(s_last, tp_of(y + d, z, c)) for d in range(1, ny)]
    for peer in peers:
        pl.semaphore_signal(barrier, inc=1, device_id=peer, device_id_type=MESH)

    for one in loads[:5]:
        one.wait()

    spread_at = lax.broadcasted_iota(jnp.int32, (4, 256), 1) // 64
    spread_of = lax.broadcasted_iota(jnp.int32, (4, 256), 0)
    spread = jnp.where(spread_at == spread_of, 1.0, 0.0).astype(BF)
    for raw, wide in ((gm, gme), (um, ume)):
        wide[...] = lax.dot_general(
            raw[...].astype(BF),
            spread,
            (((0,), (0,)), ((), ())),
            preferred_element_type=F32,
        )

    def mask_up(weight, wide):
        @pl.loop(0, feats // 64, unroll=8)
        def _(i):
            at = pl.ds(pl.multiple_of(i * 64, 64), 64)
            row = jnp.broadcast_to(wide[pl.ds(i, 1), :], (16, 256)).astype(BF)
            block = weight[at, :].reshape(4, 16, 256) * row[None]
            weight[at, :] = block.reshape(64, 256)

    loads[5].wait()
    mask_up(wg, gme)
    loads[6].wait()
    mask_up(wu, ume)

    down_bits = dm[...].astype(BF)
    entries = feats // 64
    pick_row = lax.broadcasted_iota(jnp.int32, (entries, entries), 0)
    pick_lane = lax.broadcasted_iota(jnp.int32, (entries, entries), 1)
    row_is = lax.broadcasted_iota(jnp.int32, (4, entries), 0)
    lane_is = lax.broadcasted_iota(jnp.int32, (4, entries), 1)
    turned = jnp.zeros((4, entries), F32)
    for q in range(4):
        pick = jnp.where(pick_row == pick_lane // 4 * 4 + q, 1.0, 0.0).astype(BF)
        found = jnp.dot(down_bits, pick, preferred_element_type=F32)
        found = jnp.where(row_is == lane_is % 4, found, 0.0)
        found = jnp.sum(found, axis=0, keepdims=True)
        turned = turned + jnp.where(row_is == q, found, 0.0)
    dme[...] = lax.dot_general(
        turned.astype(BF),
        spread,
        (((0,), (0,)), ((), ())),
        preferred_element_type=F32,
    )
    sort_row = lax.broadcasted_iota(jnp.int32, (256, 256), 0)
    sort_lane = lax.broadcasted_iota(jnp.int32, (256, 256), 1)
    sender = (so_v[0] // 4 + nt - t) % nt
    sender_of = jnp.zeros((1, 256), jnp.int32)
    for k in range(REACH):
        sender_of = jnp.where(
            sort_lane[:1] // 64 == k, sender[:, k : k + 1], sender_of
        )
    same = (sort_row // 64 == sender_of) & (sort_row % 64 == sort_lane % 64)
    sort = jnp.where(same, 1.0, 0.0).astype(BF)

    def mask_down(first, last):
        @pl.loop(first, last, unroll=2)
        def _(i):
            cols = pl.ds(pl.multiple_of(i * 256, 256), 256)
            blocks = []
            for k in range(REACH):
                row = dme[pl.ds(4 * i + k, 1), :]
                row = jnp.broadcast_to(row, (16, 256)).astype(BF)
                block = wd[k * 64 : (k + 1) * 64, cols]
                block = block.reshape(4, 16, 256) * row[None]
                blocks.append(block.reshape(64, 256))
            wdp[0, :, cols] = jnp.dot(
                sort, jnp.concatenate(blocks, axis=0), preferred_element_type=F32
            ).astype(BF)

    tiles_down = feats // 256
    early, middle = tiles_down * 3 // 16 * 2, tiles_down * 5 // 16 * 2
    loads[7].wait()
    mask_down(0, early)

    pl.semaphore_wait(barrier, len(peers))

    own = xbuf.at[0, 0, c]

    def z_gather(d):
        return remote(
            own, xbuf.at[0, d, c], az_ss.at[d], az_rs.at[d], s, tp_of(y, z + d, c)
        )

    def y_gather(dy, d):
        return remote(
            xbuf.at[0, d, c],
            xbuf.at[dy, d, c],
            ay_ss.at[dy, d],
            ay_rs.at[dy, d],
            s,
            tp_of(y + dy, z, c),
        )

    def p_gather(dy, d):
        return remote(
            xbuf.at[dy, d, c],
            xbuf.at[dy, d, c],
            ap_ss.at[dy, d],
            ap_rs.at[dy, d],
            s,
            partner,
        )

    keep_copy = remote(own, xprev, x_ss.at[0], x_rs.at[0], s_next, t)

    def z_scatter(p):
        return remote(
            zsend.at[p],
            zrecv.at[p],
            z_ss.at[p],
            z_rs.at[p],
            s if p // GROUP in ACROSS else s_next,
            tp_of(y, z + far[p], c),
        )

    def y_scatter(dy, g):
        some = pl.ds(g * GROUP, GROUP)
        return remote(
            ysend.at[dy, some],
            yrecv.at[dy, some],
            y_ss.at[dy, g],
            y_rs.at[dy, g],
            s_next if g in ACROSS else s,
            tp_of(y + dy, z, c),
        )

    def send_own():
        for d in far[:-1]:
            z_gather(d).start()
        for dy in y_far:
            y_gather(dy, 0).start()
        p_gather(0, 0).start()
        keep_copy.start()

    def arrive():
        for g in ACROSS:
            for dy in range(ny):
                y_scatter(dy, g).wait_recv()
            for p in range(g * GROUP, (g + 1) * GROUP):
                total = yrecv[0, p].astype(F32)
                for dy in range(1, ny):
                    total = total + yrecv[dy, p].astype(F32)
                zsend[p] = total.astype(BF)
                z_scatter(p).start()
        keep_copy.wait_recv()
        total = xprev[...].astype(F32)
        for p in range(nz):
            z_scatter(p).wait_recv()
            total = total + zrecv[p].astype(F32)
        return total.astype(BF)

    @pl.when(s == 0)
    def _():
        token_load.wait()
        send_own()

    so_copies = [
        remote(so_v.at[0], so_v.at[j], so_ss.at[j], so_rs.at[j], s, (t + j) % nt)
        for j in range(1, REACH)
    ]
    for one in so_copies:
        one.start()

    mask_down(early, middle)

    for one in so_copies:
        one.wait_recv()
    row_of = lax.broadcasted_iota(jnp.int32, (256, 128), 0)
    lane_of = lax.broadcasted_iota(jnp.int32, (256, 128), 1)
    for j in range(REACH):
        order = so_v[j]
        mine = jnp.sum(
            jnp.where(order // 4 == t, order % 4, 0), axis=1, keepdims=True
        )
        hit = (row_of == mine * 64 + lane_of % 64) & (lane_of // 64 == j % 2)
        perm[:, j * 128 : (j + 1) * 128] = jnp.where(hit, 1.0, 0.0).astype(BF)

    def move(j):
        block = pl.ds(j * 64, 64)
        return remote(
            wdp.at[0, block],
            wdp.at[1, block],
            m_ss.at[j],
            m_rs.at[j],
            s,
            (t + j) % nt,
        )

    moved = jnp.where(s >= MOVE_FROM, 1, 0)

    @pl.when(s > 0)
    def _():
        mask_down(middle, tiles_down)

    @pl.when(s >= MOVE_FROM)
    def _():
        for j in range(1, REACH):
            move(j).start()
        stay = pltpu.make_async_copy(
            wdp.at[0, pl.ds(0, 64)], wdp.at[1, pl.ds(0, 64)], m_rs.at[0]
        )
        stay.start()
        for j in range(1, REACH):
            move(j).wait()
        stay.wait()

    @pl.when(s > 0)
    def _():
        rows_in = arrive()
        xbuf[0, 0, c] = rows_in
        out_ref[...] = rows_in
        send_own()

    def block_product(d, state):
        gate, upper, squares = state
        for dy in range(ny):
            at = pos(y + ny - dy, z + nz - d)
            wide = jnp.concatenate(
                [xbuf[dy, d, 0], xbuf[dy, d, 1]], axis=1
            ).astype(F32)
            squares = squares + wide * wide
            where = pl.ds(pl.multiple_of(at * 256, 256), 256)
            left = (wide * gain[:, where]).astype(BF)
            gate = gate + jnp.dot(left, wg[where, :], preferred_element_type=F32)
            upper = upper + jnp.dot(left, wu[where, :], preferred_element_type=F32)
        return gate, upper, squares

    state = tuple(jnp.zeros((rows, 256), F32) for _ in range(3))
    for d in near[1:]:
        z_gather(d).wait_recv()
        for dy in y_far:
            y_gather(dy, d).start()
        p_gather(0, d).start()

    @pl.when(s == 0)
    def _():
        mask_down(middle, tiles_down)

    for step in range(nz + 1):
        if step < nz:
            d = near[step]
            for dy in y_far[::-1]:
                y_gather(dy, d).wait_recv()
                p_gather(dy, d).start()
        if step >= 1:
            d = near[step - 1]
            for dy in range(ny):
                remote(
                    xbuf.at[dy, d, c],
                    xbuf.at[dy, d, 1 - c],
                    ap_ss.at[dy, d],
                    ap_rs.at[dy, d],
                    s,
                    partner,
                ).wait_recv()
            state = block_product(d, state)
    gate, upper, squares = state
    scale = lax.rsqrt(jnp.sum(squares, axis=1, keepdims=True) / feats + 1e-05)
    gate = gate * scale
    hidden = (gate / (1.0 + jnp.exp(-gate)) * (upper * scale)).astype(BF)
    routed = jnp.dot(hidden, perm[...], preferred_element_type=F32).astype(BF)

    def hand_over(j):
        return remote(
            hsend.at[j], hrecv.at[j], h_ss.at[j], h_rs.at[j], s, (t + nt - j) % nt
        )

    @pl.when(s < MOVE_FROM)
    def _():
        for j in range(REACH - 1, 0, -1):
            hsend[j] = routed[:, j * 128 : (j + 1) * 128]
            hand_over(j).start()
        for j in range(1, REACH):
            hand_over(j).wait()

    @pl.when(s >= MOVE_FROM)
    def _():
        for j in range(1, REACH):
            hrecv[j] = routed[:, j * 128 : (j + 1) * 128]

    tiles = jnp.concatenate(
        [routed[:, :128] + hrecv[1], hrecv[2] + hrecv[3]], axis=1
    )

    def p_scatter(g):
        some = pl.ds(g * GROUP, GROUP)
        return remote(
            psend.at[some], precv.at[some], p_ss.at[g], p_rs.at[g], s, partner
        )

    def sum_pair(g):
        p_scatter(g).wait_recv()
        for dy in y_far + ([0] if g in ACROSS else []):
            for p in range(g * GROUP, (g + 1) * GROUP):
                ysend[dy, p] = (part[p, dy] + precv[p, dy].astype(F32)).astype(BF)
            y_scatter(dy, g).start()

    for g in range(groups):
        for p in range(g * GROUP, (g + 1) * GROUP):
            for dy in range(ny):
                at = pos(y + dy, z + far[p])
                cols = pl.ds(pl.multiple_of(at * 256, 256), 256)
                both = jnp.dot(tiles, wdp[moved, :, cols], preferred_element_type=F32)
                low, high = both[:, :128], both[:, 128:]
                part[p, dy] = jnp.where(c == 0, low, high)
                psend[p, dy] = jnp.where(c == 0, high, low).astype(BF)
        p_scatter(g).start()
        if g >= LAG:
            sum_pair(g - LAG)
    for g in range(max(groups - LAG, 0), groups):
        sum_pair(g)
    for g in range(groups):
        if g in ACROSS:
            continue
        for dy in y_far[::-1]:
            y_scatter(dy, g).wait_recv()
        for p in range(g * GROUP, (g + 1) * GROUP):
            total = part[p, 0] + precv[p, 0].astype(F32)
            for dy in range(1, ny):
                total = total + yrecv[dy, p].astype(F32)
            zsend[p] = total.astype(BF)
            z_scatter(p).start()

    @pl.when(s == 0)
    def _():
        out_ref[...] = arrive()

    for one in so_copies:
        one.wait_send()
    keep_copy.wait_send()
    for d in range(1, nz):
        z_gather(d).wait_send()
    for d in range(nz):
        for dy in range(1, ny):
            y_gather(dy, d).wait_send()
        for dy in range(ny):
            p_gather(dy, d).wait_send()
        z_scatter(d).wait_send()
    for g in range(groups):
        p_scatter(g).wait_send()
        for dy in range(0 if g in ACROSS else 1, ny):
            y_scatter(dy, g).wait_send()


def body(
    tokens,
    norm_gain,
    gate_weight,
    up_weight,
    gate_mask,
    up_mask,
    down_weight,
    down_mask,
    slot_order,
):
    sections = lax.axis_size("section")
    nt = lax.axis_size("tp")
    ny, nz = tp_grid(nt)
    rows = tokens.shape[0]
    feats = nt * 128
    groups = nz // GROUP
    dma = pltpu.SemaphoreType.DMA
    scratch = [
        pltpu.VMEM((feats, 256), BF),
        pltpu.VMEM((feats, 256), BF),
        pltpu.VMEM((256, feats), BF),
        pltpu.VMEM((2, 256, feats), BF),
        pltpu.VMEM((1, feats), F32),
        pltpu.VMEM((4, feats // 64), jnp.int32),
        pltpu.VMEM((4, feats // 64), jnp.int32),
        pltpu.VMEM((4, feats // 64), jnp.int32),
        pltpu.VMEM((REACH, 1, 4), jnp.int32),
        pltpu.VMEM((feats // 64, 256), F32),
        pltpu.VMEM((feats // 64, 256), F32),
        pltpu.VMEM((feats // 64, 256), F32),
        pltpu.VMEM((256, REACH * 128), BF),
        pltpu.VMEM((ny, nz, 2, rows, 128), BF),
        pltpu.VMEM((rows, 128), BF),
        pltpu.VMEM((REACH, rows, 128), BF),
        pltpu.VMEM((REACH, rows, 128), BF),
        pltpu.VMEM((nz, ny, rows, 128), F32),
        pltpu.VMEM((nz, ny, rows, 128), BF),
        pltpu.VMEM((nz, ny, rows, 128), BF),
        pltpu.VMEM((ny, nz, rows, 128), BF),
        pltpu.VMEM((ny, nz, rows, 128), BF),
        pltpu.VMEM((nz, rows, 128), BF),
        pltpu.VMEM((nz, rows, 128), BF),
        dma((10,)),
    ]
    for shape in (
        (REACH,),
        (nz,),
        (ny, nz),
        (ny, nz),
        (REACH,),
        (groups,),
        (ny, groups),
        (nz,),
        (1,),
        (REACH,),
    ):
        scratch += [dma(shape), dma(shape)]
    received = pl.pallas_call(
        functools.partial(kernel, sections, ny, nz),
        out_shape=jax.ShapeDtypeStruct((rows, 128), BF),
        in_specs=[pl.BlockSpec(memory_space=pl.ANY)] * 9,
        out_specs=pl.BlockSpec(memory_space=pltpu.VMEM),
        scratch_shapes=scratch,
        compiler_params=pltpu.CompilerParams(
            collective_id=0,
            has_side_effects=True,
            vmem_limit_bytes=67043328,
        ),
    )(
        tokens,
        norm_gain,
        gate_weight[0],
        up_weight[0],
        gate_mask[0].T,
        up_mask[0].T,
        down_weight[0],
        down_mask[0],
        slot_order,
    )
    return received[None]


def solution(mesh):
    return jax.shard_map(
        body,
        mesh=mesh,
        in_specs=(
            P(None, "tp"),
            P("section", None),
            P("section", None, "tp"),
            P("section", None, "tp"),
            P("section", None, "tp"),
            P("section", None, "tp"),
            P("section", "tp", None),
            P("section", "tp", None),
            P("section", "tp"),
        ),
        out_specs=P("section", None, "tp"),
        check_vma=False,
    )
```
